32 devices in a mesh: depth: 4 (over y, x), surf: 8 (over z, core).
Axes of the slice: x: 2, y: 2, z: 4, core: 2. Of those that a mesh axis runs over, the one named last changes fastest.
Arguments:
- initial_warmth: float32 [256, 32, 2048], P('depth', 'surf'), may hold values from -6 to 6
- substance_label: int32 [256], replicated, may hold values from 0 to 3, never falling along the last dimension, each value on 1 to 128 neighbouring positions
- neighbour_kernel: float32 [4, 24], replicated, may hold values from 0.004 to 0.04
- arriving_heat_rate: float32 [32, 2048], P('surf'), may hold values from -3 to 3
- implicit_inverse_operator: float32 [256, 256], replicated, may hold values from 0 to 0.61, as said below
Outputs:
- final_temperature: float32 [256, 32, 2048], P('depth', 'surf')
The draws below stay inside these ranges and needn't reach their ends.
Inputs may be any that keep to these rules, and one draw needn't show every extreme that they name: `substance_label`: material numbers never fall from layer 0 (the heated side) to the last layer; every material holds at least one layer. `implicit_inverse_operator`: all entries are positive.
All inputs are finite; a program needn't handle non-finite values.
Results may differ from the reference program's by a relative error of at most 0.0001.
Values sent between devices are 32-bit elements; how exact they have to be, the bound alone decides.
A program may use at most 64 MiB of HBM per device.

```python
import math
import jax
import jax.numpy as jnp
import numpy as np
from jax import lax

L = 256
SY = 2048
STEPS = 3
NX = 32


def draw_initial_warmth(key, part):
    return jnp.clip(jax.random.normal(key, (L, NX, SY), jnp.float32), -6.0, 6.0)


def draw_implicit_inverse_operator(key, part):
    key_rough = jax.random.fold_in(key, 11)
    key_diag = jax.random.fold_in(key, 23)
    rows = jnp.arange(L)[:, None]
    cols = jnp.arange(L)[None, :]
    distance = jnp.abs(rows - cols).astype(jnp.float32)
    length_total = L / 8.0
    ratio = jnp.exp(-1.0 / length_total)
    rough = jax.random.uniform(key_rough, (L, L), jnp.float32, 0.5, 1.5)
    diag_gain = jax.random.uniform(key_diag, (L,), jnp.float32, 0.9, 1.1)
    off_part = 0.3 * rough * jnp.exp(-distance / length_total) * (1.0 - ratio) / (2.0 * ratio)
    diagonal_portion = jnp.broadcast_to(0.55 * diag_gain[:, None], (L, L))
    return jnp.where(distance == 0.0, diagonal_portion, off_part)


def block_scale(own_key, extent, shards, least, top_value):
    def one(axis_at, blocks):
        draws = jax.random.uniform(jax.random.fold_in(jax.random.fold_in(own_key, 6), axis_at), (blocks,), jnp.float32, least / len(shards), top_value / len(shards))
        return jnp.repeat(jnp.exp(draws), extent[axis_at] // blocks).reshape((-1,) + (1,) * (len(extent) - axis_at - 1))

    gain = one(*shards[0])
    for cut in shards[1:]:
        gain = gain * one(*cut)
    return gain


def length_profile(count, total, limit, lean):
    portions = [(1 << 20) // math.isqrt(grade ** lean) + 1 for grade in range(2, count + 1)]
    spare, holding = total - limit - (count - 1), [1] * (count - 1)
    while spare > 0:
        free = [i for i in range(count - 1) if holding[i] < limit]
        mass, remaining = sum([portions[i] for i in free]), spare
        for i in free:
            addition = min(limit - holding[i], max(1, remaining * portions[i] // mass), spare)
            holding[i] = holding[i] + addition
            spare = spare - addition
    return np.array([limit] + holding)


def uneven_parts(rng, count, total, most, skew):
    if count == 2:
        one = jax.random.randint(rng, (), max(1, total - most), min(most, total - 1) + 1)
        return jnp.stack([one, total - one])
    tallies = jnp.asarray(length_profile(count, total, most, skew), jnp.int32)
    couples = (count - 1) // 2
    source_of, sink = tallies[1:1 + 2 * couples:2], tallies[2:2 + 2 * couples:2]
    margin = jnp.minimum(source_of - 1, most - sink)
    passed = jax.random.randint(jax.random.fold_in(rng, 1), (couples,), 0, 1 << 20) % (margin + 1)
    tallies = tallies.at[1:1 + 2 * couples:2].set(source_of - passed).at[2:2 + 2 * couples:2].set(sink + passed)
    return tallies[jax.random.permutation(jax.random.fold_in(rng, 2), count)]


def gaussian(rng, dims, width, bound, cuts=(), kind=jnp.bfloat16):
    entries = jax.random.normal(rng, dims, jnp.float32) * width
    if len(cuts) > 0:
        entries = block_scale(rng, dims, cuts, -0.22, 0.18) * entries
    return jnp.clip(entries, min=-bound, max=bound).astype(kind)


def setup_inputs(seed: int = 0) -> dict:
    splits = jax.random.split(jax.random.key(seed), 6)
    return {
        "initial_warmth": draw_initial_warmth(jax.random.fold_in(splits[5], 71), 0),
        "substance_label": jnp.searchsorted(jnp.cumsum(uneven_parts(splits[1], 4, L, L // 2, 0)), jnp.arange(L), side="right").astype(jnp.int32),
        "neighbour_kernel": jnp.clip(jnp.exp(jax.random.uniform(splits[2], (4, 24), jnp.float32, math.log(0.004), math.log(0.04))), 0.004, 0.04),
        "arriving_heat_rate": gaussian(splits[3], (NX, SY), 0.5, 3.0, ((0, 8),), jnp.float32),
        "implicit_inverse_operator": draw_implicit_inverse_operator(jax.random.fold_in(splits[5], 71), 0),
    }


neighbours = [(row_step, column_stride) for row_step in range(-2, 3) for column_stride in range(-2, 3) if row_step != 0 or column_stride != 0]


def coefficients(substance_label, neighbour_kernel):
    chosen = (substance_label[:, None] == jnp.arange(4, dtype=jnp.int32)[None, :]).astype(neighbour_kernel.dtype)
    return jnp.sum(chosen[:, :, None] * neighbour_kernel[None, :, :], axis=1)


def sheet_diffusion(operands):
    plane, kernel_factors = operands
    bordered_field = jnp.pad(plane, 2)
    tally_lines, grid_breadth = plane.shape
    accumulated = jnp.zeros_like(plane)
    for place_index, offset in enumerate(neighbours):
        displaced_field = bordered_field[2 + offset[0]:2 + offset[0] + tally_lines, 2 + offset[1]:2 + offset[1] + grid_breadth]
        accumulated = accumulated + kernel_factors[place_index] * (displaced_field - plane)
    return plane + accumulated


def reference(initial_warmth, substance_label, neighbour_kernel, arriving_heat_rate, implicit_inverse_operator):
    sheet_factors = coefficients(substance_label, neighbour_kernel)
    current_thermal_state = initial_warmth
    for step_index in range(STEPS):
        advance_explicit_step = lax.map(sheet_diffusion, (current_thermal_state, sheet_factors))
        advance_explicit_step = advance_explicit_step.at[0].add(arriving_heat_rate)
        current_thermal_state = jnp.einsum("mq,qhl->mhl", implicit_inverse_operator, advance_explicit_step, precision=lax.Precision.HIGHEST)
    return current_thermal_state
```

```python
import functools

import jax
import jax.numpy as jnp
from jax import lax
from jax.experimental import pallas as pl
from jax.experimental.pallas import tpu as pltpu
from jax.sharding import PartitionSpec as P

LANES = 128
REACH = 6
MESH = pl.DeviceIdType.MESH


def flipped(rank, mask, count):
    out, bit = 0, 1
    while bit < count:
        mine = (rank // bit) % 2
        out = out + bit * ((1 - mine) if (mask // bit) % 2 else mine)
        bit *= 2
    return out


def kernel(
    nd, ns, tiles,
    x_ref, lab_ref, nk_ref, heat_ref, op_ref, out_ref,
    raw, eraw, eb, hb, s0, s1, s2, ex, ob, coef, op3,
    a_send, a_recv, a_loc, z_send, z_recv, ze_send, ze_recv,
    h_send, h_recv, x_send, x_recv, o_send, o_recv, o_loc,
):
    d = lax.axis_index("depth")
    s = lax.axis_index("surf")
    layers_here = x_ref.shape[0]
    layers = op_ref.shape[0]
    width = heat_ref.shape[1]
    cols = tiles * LANES
    ring = tiles + 1
    peers = [j for j in range(nd - 1, 0, -1)]
    has = (s > 0, s < ns - 1)
    near = (s - 1, s + 1)
    mine = pl.ds(pl.multiple_of(d * layers_here, 8), layers_here)

    barrier = pltpu.get_barrier_semaphore()
    for j in peers:
        pl.semaphore_signal(
            barrier, inc=1, device_id={"depth": flipped(d, j, nd)}, device_id_type=MESH
        )
    for side in range(2):
        @pl.when(has[side])
        def _():
            pl.semaphore_signal(
                barrier, inc=1, device_id={"surf": near[side]}, device_id_type=MESH
            )
    at_end = jnp.where(s > 0, 0, 1) + jnp.where(s < ns - 1, 0, 1)
    pl.semaphore_wait(barrier, nd + 1 - at_end)

    def block_cols(b, t):
        return pl.ds(pl.multiple_of(b * cols + t * LANES, LANES), LANES)

    def spread(j, t):
        p = flipped(d, j, nd)
        if t == tiles:
            src, dst = eb.at[p], eraw.at[1, mine]
        else:
            src, dst = x_ref.at[:, :, block_cols(p, t)], raw.at[1, t, mine]
        return pltpu.make_async_remote_copy(
            src, dst, a_send.at[j, t], a_recv.at[j, t],
            device_id={"depth": p}, device_id_type=MESH,
        )

    def keep(t):
        if t == tiles:
            return pltpu.make_async_copy(eb.at[d], eraw.at[1, mine], a_loc.at[t])
        return pltpu.make_async_copy(
            x_ref.at[:, :, block_cols(d, t)], raw.at[1, t, mine], a_loc.at[t]
        )

    def forward(side, t):
        if t == tiles:
            src, dst = eraw.at[1], eraw.at[2 - 2 * side]
            snd, rcv = ze_send.at[side], ze_recv.at[side]
        else:
            src, dst = raw.at[1, t], raw.at[2 - 2 * side, t]
            snd, rcv = z_send.at[side, t], z_recv.at[side, t]
        return pltpu.make_async_remote_copy(
            src, dst, snd, rcv, device_id={"surf": near[side]}, device_id_type=MESH
        )

    def heat_out(side):
        return pltpu.make_async_remote_copy(
            heat_ref, hb.at[1 - side], h_send.at[side], h_recv.at[side],
            device_id={"surf": near[side]}, device_id_type=MESH,
        )

    def trade(side, t):
        return pltpu.make_async_remote_copy(
            s2.at[t, pl.ds(2 + 2 * side, 2)], s2.at[t, pl.ds(6 - 6 * side, 2)],
            x_send.at[side, t], x_recv.at[side, t],
            device_id={"surf": near[side]}, device_id_type=MESH,
        )

    def give_back(j, t):
        p = flipped(d, j, nd)
        theirs = pl.ds(pl.multiple_of(p * layers_here, 8), layers_here)
        return pltpu.make_async_remote_copy(
            ob.at[t, theirs], out_ref.at[:, :, block_cols(d, t)],
            o_send.at[j, t], o_recv.at[j, t],
            device_id={"depth": p}, device_id_type=MESH,
        )

    def put_home(t):
        return pltpu.make_async_copy(
            ob.at[t, mine], out_ref.at[:, :, block_cols(d, t)], o_loc.at[t]
        )

    for j in peers:
        spread(j, 0).start()
    lane8 = lax.broadcasted_iota(jnp.int32, (8, LANES), 1)
    for b in range(nd):
        @pl.loop(0, layers_here // 8)
        def _(g):
            rows = pl.ds(pl.multiple_of(g * 8, 8), 8)
            packed = jnp.zeros((8, LANES), jnp.float32)
            for r in range(4):
                edge = jnp.zeros((8, LANES), jnp.float32)
                if b < nd - 1:
                    ahead = x_ref[rows, r, (b + 1) * cols:(b + 1) * cols + LANES]
                    edge = jnp.where(lane8 < REACH, ahead, edge)
                if b > 0:
                    behind = x_ref[rows, r, b * cols - LANES:b * cols]
                    edge = jnp.where(lane8 >= LANES - REACH, behind, edge)
                packed = packed + (pltpu.roll(edge, 16 * r, 1) if r else edge)
            eb[b, rows, :] = packed
    for t in [tiles] + list(range(1, tiles)):
        for j in peers:
            spread(j, t).start()
    for t in range(ring):
        keep(t).start()
    for side in range(2):
        @pl.when(has[side])
        def _():
            heat_out(side).start()

    @pl.loop(0, layers // 8)
    def _(g):
        rows = pl.ds(pl.multiple_of(g * 8, 8), 8)
        lab = lab_ref[rows, :]
        is0, is1, is2 = lab == 0, lab == 1, lab == 2
        total = jnp.zeros((8, LANES), jnp.float32)
        for k in range(24):
            c = jnp.where(
                is0, nk_ref[0, k],
                jnp.where(is1, nk_ref[1, k], jnp.where(is2, nk_ref[2, k], nk_ref[3, k])),
            )
            coef[k if k < 12 else k + 1, rows, :] = c
            total = total + c
        coef[12, rows, :] = 1.0 - total

    high = op_ref[...].astype(jnp.bfloat16)
    op3[:, 0:layers] = high
    op3[:, layers:2 * layers] = high
    op3[:, 2 * layers:] = (op_ref[...] - high.astype(jnp.float32)).astype(jnp.bfloat16)

    for side in range(2):
        @pl.when(jnp.logical_not(has[side]))
        def _():
            for t in range(ring):
                for r in range(2):
                    s2[t, 6 * side + r, :, :] = jnp.zeros((layers, LANES), jnp.float32)
                for r in range(4):
                    s0[t, 8 * side + r, :, :] = jnp.zeros((layers, LANES), jnp.float32)
            hb[side, :, :] = jnp.zeros((4, width), jnp.float32)

    for side in range(2):
        @pl.when(has[side])
        def _():
            heat_out(side).wait_send()
            heat_out(1 - side).wait_recv()

    row_keep = [jnp.where(h, 1.0, 0.0).astype(jnp.float32) for h in has]
    lane1 = lax.broadcasted_iota(jnp.int32, (1, LANES), 1)
    edge_keep = jnp.where(
        lane1 < REACH, jnp.where(d < nd - 1, 1.0, 0.0),
        jnp.where(lane1 >= LANES - REACH, jnp.where(d > 0, 1.0, 0.0), 0.0),
    ).astype(jnp.float32)

    def heat_row(row, t):
        if row < 0:
            src, r = hb.at[0], row + 4
        elif row > 3:
            src, r = hb.at[1], row - 4
        else:
            src, r = heat_ref, row
        if t < tiles:
            return src[r:r + 1, block_cols(d, t)]
        ahead = src[r:r + 1, block_cols(lax.rem(d + 1, nd), 0)]
        behind = src[r:r + 1, block_cols(lax.rem(d + nd - 1, nd), tiles - 1)]
        return jnp.where(lane1 < REACH, ahead, behind)

    def lateral(src, t, made, first):
        left, right = (t - 1) % ring, (t + 1) % ring

        @pl.loop(0, layers // 8)
        def _(g):
            rows = pl.ds(pl.multiple_of(g * 8, 8), 8)
            cs = [coef[k, rows, :] for k in range(25)]
            acc = [None] * made
            for i in range(made + 4):
                mid, lo, hi = src[t, i, rows, :], src[left, i, rows, :], src[right, i, rows, :]
                views = [
                    pltpu.roll(jnp.where(lane8 >= LANES - 2, lo, mid), 2, 1),
                    pltpu.roll(jnp.where(lane8 >= LANES - 1, lo, mid), 1, 1),
                    mid,
                    pltpu.roll(jnp.where(lane8 < 1, hi, mid), LANES - 1, 1),
                    pltpu.roll(jnp.where(lane8 < 2, hi, mid), LANES - 2, 1),
                ]
                for r in range(max(0, i - 4), min(made, i + 1)):
                    for q in range(5):
                        term = cs[(i - r) * 5 + q] * views[q]
                        acc[r] = term if acc[r] is None else acc[r] + term
            for r in range(made):
                ex[rows, r * LANES:(r + 1) * LANES] = acc[r]

        top = lax.broadcasted_iota(jnp.int32, (8, LANES), 0) == 0
        for r in range(made):
            lanes = slice(r * LANES, (r + 1) * LANES)
            heat = jnp.broadcast_to(heat_row(first + r, t), (8, LANES))
            ex[0:8, lanes] = ex[0:8, lanes] + jnp.where(top, heat, 0.0)

    def implicit(t, made, first, store):
        for pair in range(made // 2):
            e = ex[:, pair * 2 * LANES:(pair + 1) * 2 * LANES]
            if first < 0 and pair == 0:
                e = e * row_keep[0]
            if first < 0 and pair == made // 2 - 1:
                e = e * row_keep[1]
            if t == tiles:
                e = e * jnp.concatenate([edge_keep, edge_keep], axis=1)
            eh = e.astype(jnp.bfloat16)
            el = (e - eh.astype(jnp.float32)).astype(jnp.bfloat16)
            y = jnp.dot(
                op3[...], jnp.concatenate([eh, el, eh], axis=0),
                preferred_element_type=jnp.float32,
            )
            store(2 * pair, y[:, :LANES])
            store(2 * pair + 1, y[:, LANES:])

    done = set()
    arrival = [0, tiles] + list(range(1, tiles))

    def once(f):
        def g(t):
            if (f.__name__, t) not in done:
                done.add((f.__name__, t))
                f(t)
        return g

    @once
    def arrive(t):
        at = arrival.index(t)
        if at:
            arrive(arrival[at - 1])
        for j in peers:
            spread(j, t).wait_recv()
        keep(t).wait()
        for side in range(2):
            @pl.when(has[side])
            def _():
                forward(side, t).start()

    @once
    def unpack(t):
        at = arrival.index(t)
        arrive(arrival[min(at + 1, tiles)])

        def relayout(part):
            if t == tiles:
                @pl.loop(0, layers // 8)
                def _(g):
                    rows = pl.ds(pl.multiple_of(g * 8, 8), 8)
                    packed = eraw[part, rows, :]
                    wanted = jnp.logical_or(lane8 < REACH, lane8 >= LANES - REACH)
                    for r in range(4):
                        v = pltpu.roll(packed, LANES - 16 * r, 1) if r else packed
                        s0[t, 4 * part + r, rows, :] = jnp.where(wanted, v, 0.0)
            else:
                @pl.loop(0, layers // 8)
                def _(g):
                    rows = pl.ds(pl.multiple_of(g * 8, 8), 8)
                    for r in range(4):
                        s0[t, 4 * part + r, rows, :] = raw[part, t, rows, r, :]

        relayout(1)
        for side in range(2):
            @pl.when(has[side])
            def _():
                forward(1 - side, t).wait_recv()
                relayout(2 * side)

    @once
    def step1(t):
        for u in (t, (t - 1) % ring, (t + 1) % ring):
            unpack(u)
        lateral(s0, t, 8, -2)

        def store(r, y):
            s1[t, r, :, :] = y
        implicit(t, 8, -2, store)

    @once
    def step2(t):
        for u in ((t - 1) % ring, t, (t + 1) % ring):
            step1(u)
        lateral(s1, t, 4, 0)

        def store(r, y):
            s2[t, 2 + r, :, :] = y
        implicit(t, 4, 0, store)
        for side in range(2):
            @pl.when(has[side])
            def _():
                trade(side, t).start()

    @once
    def halo(t):
        for side in range(2):
            @pl.when(has[side])
            def _():
                trade(1 - side, t).wait_recv()

    @once
    def step3(t):
        around = (t, (t - 1) % ring, (t + 1) % ring)
        for u in around:
            step2(u)
        for u in around:
            halo(u)
        lateral(s2, t, 4, 0)

        def store(r, y):
            ob[t, :, r, :] = y
        implicit(t, 4, 0, store)
        for j in peers:
            give_back(j, t).start()
        put_home(t).start()

    order = list(range(1, tiles)) + [0]
    for t in order:
        step3(t)

    for t in order:
        for j in peers:
            give_back(j, t).wait()
        put_home(t).wait()
    for t in range(ring):
        for j in peers:
            spread(j, t).wait_send()
        for side in range(2):
            @pl.when(has[side])
            def _():
                forward(side, t).wait_send()
                trade(side, t).wait_send()


def shards(
    nd, ns,
    initial_warmth, substance_label, neighbour_kernel, arriving_heat_rate, implicit_inverse_operator,
):
    layers_here, rows, width = initial_warmth.shape
    layers = implicit_inverse_operator.shape[0]
    tiles = width // nd // LANES
    ring = tiles + 1
    labels = jnp.broadcast_to(substance_label[:, None], (layers, LANES))
    f32, dma = jnp.float32, pltpu.SemaphoreType.DMA
    vmem = pl.BlockSpec(memory_space=pltpu.VMEM)
    return pl.pallas_call(
        functools.partial(kernel, nd, ns, tiles),
        out_shape=jax.ShapeDtypeStruct(initial_warmth.shape, f32),
        in_specs=[vmem, vmem, pl.BlockSpec(memory_space=pltpu.SMEM), vmem, vmem],
        out_specs=pl.BlockSpec(memory_space=pl.ANY),
        scratch_shapes=[
            pltpu.VMEM((3, tiles, layers, rows, LANES), f32),
            pltpu.VMEM((3, layers, LANES), f32),
            pltpu.VMEM((nd, layers_here, LANES), f32),
            pltpu.VMEM((2, rows, width), f32),
            pltpu.VMEM((ring, 3 * rows, layers, LANES), f32),
            pltpu.VMEM((ring, 2 * rows, layers, LANES), f32),
            pltpu.VMEM((ring, 2 * rows, layers, LANES), f32),
            pltpu.VMEM((layers, 2 * rows * LANES), f32),
            pltpu.VMEM((tiles, layers, rows, LANES), f32),
            pltpu.VMEM((25, layers, LANES), f32),
            pltpu.VMEM((layers, 3 * layers), jnp.bfloat16),
            dma((nd, ring)), dma((nd, ring)), dma((ring,)),
            dma((2, tiles)), dma((2, tiles)), dma((2,)), dma((2,)),
            dma((2,)), dma((2,)), dma((2, ring)), dma((2, ring)),
            dma((nd, tiles)), dma((nd, tiles)), dma((tiles,)),
        ],
        compiler_params=pltpu.CompilerParams(
            collective_id=0, has_side_effects=True, vmem_limit_bytes=60 * 1024 * 1024
        ),
    )(initial_warmth, labels, neighbour_kernel, arriving_heat_rate, implicit_inverse_operator)


def solution(mesh):
    return jax.shard_map(
        functools.partial(shards, mesh.shape["depth"], mesh.shape["surf"]),
        mesh=mesh,
        in_specs=(P("depth", "surf", None), P(), P(), P("surf", None), P()),
        out_specs=P("depth", "surf", None),
        check_vma=False,
    )
```

```python
import functools

import jax
import jax.numpy as jnp
from jax import lax
from jax.experimental import pallas as pl
from jax.experimental.pallas import tpu as pltpu
from jax.sharding import PartitionSpec as P

LANES = 128
REACH = 6
MESH = pl.DeviceIdType.MESH


def flipped(rank, mask, count):
    out, bit = 0, 1
    while bit < count:
        mine = (rank // bit) % 2
        out = out + bit * ((1 - mine) if (mask // bit) % 2 else mine)
        bit *= 2
    return out


def kernel(
    nd, ns, tiles,
    x_ref, lab_ref, nk_ref, heat_ref, op_ref, out_ref,
    raw, eraw, eb, hb, s0, s1, s2, ex, ob, coef, op3, lab,
    a_send, a_recv, a_loc, z_send, z_recv,
    h_send, h_recv, x_send, x_recv, o_send, o_recv, o_loc,
):
    d = lax.axis_index("depth")
    s = lax.axis_index("surf")
    layers_here = x_ref.shape[0]
    layers = op_ref.shape[0]
    width = heat_ref.shape[1]
    cols = tiles * LANES
    ring = tiles + 1
    peers = [j for j in range(nd - 1, 0, -1)]
    has = (s > 0, s < ns - 1)
    near = (s - 1, s + 1)
    mine = pl.ds(pl.multiple_of(d * layers_here, 8), layers_here)

    barrier = pltpu.get_barrier_semaphore()
    for j in peers:
        pl.semaphore_signal(
            barrier, inc=1, device_id={"depth": flipped(d, j, nd)}, device_id_type=MESH
        )
    for side in range(2):
        @pl.when(has[side])
        def _():
            pl.semaphore_signal(
                barrier, inc=1, device_id={"surf": near[side]}, device_id_type=MESH
            )
    at_end = jnp.where(s > 0, 0, 1) + jnp.where(s < ns - 1, 0, 1)
    pl.semaphore_wait(barrier, nd + 1 - at_end)

    def block_cols(b, t):
        return pl.ds(pl.multiple_of(b * cols + t * LANES, LANES), LANES)

    def spread(j, t):
        p = flipped(d, j, nd)
        if t == tiles:
            src, dst = eb.at[p], eraw.at[1, mine]
        else:
            src, dst = x_ref.at[:, :, block_cols(p, t)], raw.at[1, t, mine]
        return pltpu.make_async_remote_copy(
            src, dst, a_send.at[j, t], a_recv.at[j, t],
            device_id={"depth": p}, device_id_type=MESH,
        )

    def keep(t):
        if t == tiles:
            return pltpu.make_async_copy(eb.at[d], eraw.at[1, mine], a_loc.at[t])
        return pltpu.make_async_copy(
            x_ref.at[:, :, block_cols(d, t)], raw.at[1, t, mine], a_loc.at[t]
        )

    def forward(side, j, t):
        p = flipped(d, j, nd)
        part = pl.ds(pl.multiple_of(p * layers_here, 8), layers_here)
        if t == tiles:
            src, dst = eb.at[d] if j == 0 else eraw.at[1, part], eraw.at[2 - 2 * side, part]
        else:
            src = x_ref.at[:, :, block_cols(d, t)] if j == 0 else raw.at[1, t, part]
            dst = raw.at[2 - 2 * side, t, part]
        return pltpu.make_async_remote_copy(
            src, dst, z_send.at[side, j, t], z_recv.at[side, j, t],
            device_id={"surf": near[side]}, device_id_type=MESH,
        )

    def forward_both(j, t):
        for side in range(2):
            @pl.when(has[side])
            def _():
                forward(side, j, t).start()

    def heat_out(side):
        return pltpu.make_async_remote_copy(
            heat_ref, hb.at[1 - side], h_send.at[side], h_recv.at[side],
            device_id={"surf": near[side]}, device_id_type=MESH,
        )

    def trade(side, t):
        return pltpu.make_async_remote_copy(
            s2.at[t, pl.ds(2 + 2 * side, 2)], s2.at[t, pl.ds(6 - 6 * side, 2)],
            x_send.at[side, t], x_recv.at[side, t],
            device_id={"surf": near[side]}, device_id_type=MESH,
        )

    def give_back(j, t):
        p = flipped(d, j, nd)
        theirs = pl.ds(pl.multiple_of(p * layers_here, 8), layers_here)
        return pltpu.make_async_remote_copy(
            ob.at[t, theirs], out_ref.at[:, :, block_cols(d, t)],
            o_send.at[j, t], o_recv.at[j, t],
            device_id={"depth": p}, device_id_type=MESH,
        )

    def put_home(t):
        return pltpu.make_async_copy(
            ob.at[t, mine], out_ref.at[:, :, block_cols(d, t)], o_loc.at[t]
        )

    for j in peers:
        spread(j, 0).start()
    forward_both(0, 0)
    lane8 = lax.broadcasted_iota(jnp.int32, (8, LANES), 1)
    for b in range(nd):
        @pl.loop(0, layers_here // 8)
        def _(g):
            rows = pl.ds(pl.multiple_of(g * 8, 8), 8)
            packed = jnp.zeros((8, LANES), jnp.float32)
            for r in range(4):
                edge = jnp.zeros((8, LANES), jnp.float32)
                if b < nd - 1:
                    ahead = x_ref[rows, r, (b + 1) * cols:(b + 1) * cols + LANES]
                    edge = jnp.where(lane8 < REACH, ahead, edge)
                if b > 0:
                    behind = x_ref[rows, r, b * cols - LANES:b * cols]
                    edge = jnp.where(lane8 >= LANES - REACH, behind, edge)
                packed = packed + (pltpu.roll(edge, 16 * r, 1) if r else edge)
            eb[b, rows, :] = packed
    for t in [tiles] + list(range(1, tiles)):
        for j in peers:
            spread(j, t).start()
        forward_both(0, t)
    for t in range(ring):
        keep(t).start()
    for side in range(2):
        @pl.when(has[side])
        def _():
            heat_out(side).start()

    for b in range(layers // LANES):
        row = lab_ref[:, b * LANES:(b + 1) * LANES].astype(jnp.float32)
        tall = jnp.transpose(jnp.broadcast_to(row, (LANES, LANES)))
        lab[b * LANES:(b + 1) * LANES, :] = tall

    @pl.loop(0, layers // 8)
    def _(g):
        rows = pl.ds(pl.multiple_of(g * 8, 8), 8)
        kind = lab[rows, :]
        is0, is1, is2 = kind < 0.5, kind < 1.5, kind < 2.5
        total = jnp.zeros((8, LANES), jnp.float32)
        for k in range(24):
            c = jnp.where(
                is0, nk_ref[0, k],
                jnp.where(is1, nk_ref[1, k], jnp.where(is2, nk_ref[2, k], nk_ref[3, k])),
            )
            coef[k if k < 12 else k + 1, rows, :] = c
            total = total + c
        coef[12, rows, :] = 1.0 - total

    high = op_ref[...].astype(jnp.bfloat16)
    op3[:, 0:layers] = high
    op3[:, layers:2 * layers] = high
    op3[:, 2 * layers:] = (op_ref[...] - high.astype(jnp.float32)).astype(jnp.bfloat16)

    for side in range(2):
        @pl.when(jnp.logical_not(has[side]))
        def _():
            for t in range(ring):
                for r in range(2):
                    s2[t, 6 * side + r, :, :] = jnp.zeros((layers, LANES), jnp.float32)
                for r in range(4):
                    s0[t, 8 * side + r, :, :] = jnp.zeros((layers, LANES), jnp.float32)
            hb[side, :, :] = jnp.zeros((4, width), jnp.float32)

    for side in range(2):
        @pl.when(has[side])
        def _():
            heat_out(side).wait_send()
            heat_out(1 - side).wait_recv()

    row_keep = [jnp.where(h, 1.0, 0.0).astype(jnp.float32) for h in has]
    lane1 = lax.broadcasted_iota(jnp.int32, (1, LANES), 1)
    edge_keep = jnp.where(
        lane1 < REACH, jnp.where(d < nd - 1, 1.0, 0.0),
        jnp.where(lane1 >= LANES - REACH, jnp.where(d > 0, 1.0, 0.0), 0.0),
    ).astype(jnp.float32)

    def heat_row(row, t):
        if row < 0:
            src, r = hb.at[0], row + 4
        elif row > 3:
            src, r = hb.at[1], row - 4
        else:
            src, r = heat_ref, row
        if t < tiles:
            return src[r:r + 1, block_cols(d, t)]
        ahead = src[r:r + 1, block_cols(lax.rem(d + 1, nd), 0)]
        behind = src[r:r + 1, block_cols(lax.rem(d + nd - 1, nd), tiles - 1)]
        return jnp.where(lane1 < REACH, ahead, behind)

    def lateral(src, t, made, first):
        left, right = (t - 1) % ring, (t + 1) % ring

        @pl.loop(0, layers // 8)
        def _(g):
            rows = pl.ds(pl.multiple_of(g * 8, 8), 8)
            acc = [None] * made
            for q in (2, 1, 3, 0, 4):
                cs = [coef[p * 5 + q, rows, :] for p in range(5)]
                for i in range(made + 4):
                    view = src[t, i, rows, :]
                    if q < 2:
                        view = jnp.where(lane8 >= LANES - 2 + q, src[left, i, rows, :], view)
                        view = pltpu.roll(view, 2 - q, 1)
                    elif q > 2:
                        view = jnp.where(lane8 < q - 2, src[right, i, rows, :], view)
                        view = pltpu.roll(view, LANES + 2 - q, 1)
                    for r in range(max(0, i - 4), min(made, i + 1)):
                        term = cs[i - r] * view
                        acc[r] = term if acc[r] is None else acc[r] + term
            for r in range(made):
                ex[rows, r * LANES:(r + 1) * LANES] = acc[r]

        top = lax.broadcasted_iota(jnp.int32, (8, LANES), 0) == 0
        for r in range(made):
            lanes = slice(r * LANES, (r + 1) * LANES)
            heat = jnp.broadcast_to(heat_row(first + r, t), (8, LANES))
            ex[0:8, lanes] = ex[0:8, lanes] + jnp.where(top, heat, 0.0)

    def implicit(t, made, first, store):
        for pair in range(made // 2):
            e = ex[:, pair * 2 * LANES:(pair + 1) * 2 * LANES]
            if first < 0 and pair == 0:
                e = e * row_keep[0]
            if first < 0 and pair == made // 2 - 1:
                e = e * row_keep[1]
            if t == tiles:
                e = e * jnp.concatenate([edge_keep, edge_keep], axis=1)
            eh = e.astype(jnp.bfloat16)
            el = (e - eh.astype(jnp.float32)).astype(jnp.bfloat16)
            y = jnp.dot(
                op3[...], jnp.concatenate([eh, el, eh], axis=0),
                preferred_element_type=jnp.float32,
            )
            store(2 * pair, y[:, :LANES])
            store(2 * pair + 1, y[:, LANES:])

    done = set()
    arrival = [0, tiles] + list(range(1, tiles))

    def once(f):
        def g(t):
            if (f.__name__, t) not in done:
                done.add((f.__name__, t))
                f(t)
        return g

    @once
    def arrive(t):
        at = arrival.index(t)
        if at:
            arrive(arrival[at - 1])
        for j in peers:
            spread(j, t).wait_recv()
            forward_both(j, t)
        keep(t).wait()

    @once
    def unpack(t):
        at = arrival.index(t)
        arrive(arrival[min(at + 1, tiles)])

        def relayout(part):
            if t == tiles:
                @pl.loop(0, layers // 8)
                def _(g):
                    rows = pl.ds(pl.multiple_of(g * 8, 8), 8)
                    packed = eraw[part, rows, :]
                    wanted = jnp.logical_or(lane8 < REACH, lane8 >= LANES - REACH)
                    for r in range(4):
                        v = pltpu.roll(packed, LANES - 16 * r, 1) if r else packed
                        s0[t, 4 * part + r, rows, :] = jnp.where(wanted, v, 0.0)
            else:
                @pl.loop(0, layers // 8)
                def _(g):
                    rows = pl.ds(pl.multiple_of(g * 8, 8), 8)
                    for r in range(4):
                        s0[t, 4 * part + r, rows, :] = raw[part, t, rows, r, :]

        relayout(1)
        for side in range(2):
            @pl.when(has[side])
            def _():
                for j in range(nd):
                    forward(1 - side, j, t).wait_recv()
                relayout(2 * side)

    @once
    def step1(t):
        for u in (t, (t - 1) % ring, (t + 1) % ring):
            unpack(u)
        lateral(s0, t, 8, -2)

        def store(r, y):
            s1[t, r, :, :] = y
        implicit(t, 8, -2, store)

    @once
    def step2(t):
        for u in ((t - 1) % ring, t, (t + 1) % ring):
            step1(u)
        lateral(s1, t, 4, 0)

        def store(r, y):
            s2[t, 2 + r, :, :] = y
        implicit(t, 4, 0, store)
        for side in range(2):
            @pl.when(has[side])
            def _():
                trade(side, t).start()

    @once
    def halo(t):
        for side in range(2):
            @pl.when(has[side])
            def _():
                trade(1 - side, t).wait_recv()

    @once
    def step3(t):
        around = (t, (t - 1) % ring, (t + 1) % ring)
        for u in around:
            step2(u)
        for u in around:
            halo(u)
        lateral(s2, t, 4, 0)

        def store(r, y):
            ob[t, :, r, :] = y
        implicit(t, 4, 0, store)
        for j in peers:
            give_back(j, t).start()
        put_home(t).start()

    order = list(range(1, tiles)) + [0]
    for t in order:
        step3(t)

    for t in order:
        for j in peers:
            give_back(j, t).wait()
        put_home(t).wait()
    for t in range(ring):
        for j in peers:
            spread(j, t).wait_send()
        for side in range(2):
            @pl.when(has[side])
            def _():
                for j in range(nd):
                    forward(side, j, t).wait_send()
                trade(side, t).wait_send()


def shards(
    nd, ns,
    initial_warmth, substance_label, neighbour_kernel, arriving_heat_rate, implicit_inverse_operator,
):
    layers_here, rows, width = initial_warmth.shape
    layers = implicit_inverse_operator.shape[0]
    tiles = width // nd // LANES
    ring = tiles + 1
    labels = substance_label[None, :]
    f32, dma = jnp.float32, pltpu.SemaphoreType.DMA
    vmem = pl.BlockSpec(memory_space=pltpu.VMEM)
    return pl.pallas_call(
        functools.partial(kernel, nd, ns, tiles),
        out_shape=jax.ShapeDtypeStruct(initial_warmth.shape, f32),
        in_specs=[vmem, vmem, pl.BlockSpec(memory_space=pltpu.SMEM), vmem, vmem],
        out_specs=pl.BlockSpec(memory_space=pl.ANY),
        scratch_shapes=[
            pltpu.VMEM((3, tiles, layers, rows, LANES), f32),
            pltpu.VMEM((3, layers, LANES), f32),
            pltpu.VMEM((nd, layers_here, LANES), f32),
            pltpu.VMEM((2, rows, width), f32),
            pltpu.VMEM((ring, 3 * rows, layers, LANES), f32),
            pltpu.VMEM((ring, 2 * rows, layers, LANES), f32),
            pltpu.VMEM((ring, 2 * rows, layers, LANES), f32),
            pltpu.VMEM((layers, 2 * rows * LANES), f32),
            pltpu.VMEM((tiles, layers, rows, LANES), f32),
            pltpu.VMEM((25, layers, LANES), f32),
            pltpu.VMEM((layers, 3 * layers), jnp.bfloat16),
            pltpu.VMEM((layers, LANES), f32),
            dma((nd, ring)), dma((nd, ring)), dma((ring,)),
            dma((2, nd, ring)), dma((2, nd, ring)),
            dma((2,)), dma((2,)), dma((2, ring)), dma((2, ring)),
            dma((nd, tiles)), dma((nd, tiles)), dma((tiles,)),
        ],
        compiler_params=pltpu.CompilerParams(
            collective_id=0, has_side_effects=True, vmem_limit_bytes=60 * 1024 * 1024
        ),
    )(initial_warmth, labels, neighbour_kernel, arriving_heat_rate, implicit_inverse_operator)


def solution(mesh):
    return jax.shard_map(
        functools.partial(shards, mesh.shape["depth"], mesh.shape["surf"]),
        mesh=mesh,
        in_specs=(P("depth", "surf", None), P(), P(), P("surf", None), P()),
        out_specs=P("depth", "surf", None),
        check_vma=False,
    )
```

```python
import functools

import jax
import jax.numpy as jnp
from jax import lax
from jax.experimental import pallas as pl
from jax.experimental.pallas import tpu as pltpu
from jax.sharding import PartitionSpec as P

LANES = 128
REACH = 6
MESH = pl.DeviceIdType.MESH


def flipped(rank, mask, count):
    out, bit = 0, 1
    while bit < count:
        mine = (rank // bit) % 2
        out = out + bit * ((1 - mine) if (mask // bit) % 2 else mine)
        bit *= 2
    return out


def kernel(
    nd, ns, tiles,
    x_ref, lab_ref, nk_ref, heat_ref, op_ref, out_ref,
    raw, eraw, eb, hb, s0, s1, s2, ex, ob, coef, op3, lab,
    a_send, a_recv, a_loc, z_send, z_recv,
    h_send, h_recv, x_send, x_recv, o_send, o_recv, o_loc,
):
    d = lax.axis_index("depth")
    s = lax.axis_index("surf")
    layers_here = x_ref.shape[0]
    layers = op_ref.shape[0]
    width = heat_ref.shape[1]
    cols = tiles * LANES
    ring = tiles + 1
    peers = [j for j in range(nd - 1, 0, -1)]
    has = (s > 0, s < ns - 1)
    near = (s - 1, s + 1)
    mine = pl.ds(pl.multiple_of(d * layers_here, 8), layers_here)

    barrier = pltpu.get_barrier_semaphore()
    for j in peers:
        pl.semaphore_signal(
            barrier, inc=1, device_id={"depth": flipped(d, j, nd)}, device_id_type=MESH
        )
    for side in range(2):
        @pl.when(has[side])
        def _():
            pl.semaphore_signal(
                barrier, inc=1, device_id={"surf": near[side]}, device_id_type=MESH
            )
    at_end = jnp.where(s > 0, 0, 1) + jnp.where(s < ns - 1, 0, 1)
    pl.semaphore_wait(barrier, nd + 1 - at_end)

    def block_cols(b, t):
        return pl.ds(pl.multiple_of(b * cols + t * LANES, LANES), LANES)

    def spread(j, t):
        p = flipped(d, j, nd)
        if t == tiles:
            src, dst = eb.at[p], eraw.at[1, mine]
        else:
            src, dst = x_ref.at[:, :, block_cols(p, t)], raw.at[1, t, mine]
        return pltpu.make_async_remote_copy(
            src, dst, a_send.at[j, t], a_recv.at[j, t],
            device_id={"depth": p}, device_id_type=MESH,
        )

    def keep(t):
        if t == tiles:
            return pltpu.make_async_copy(eb.at[d], eraw.at[1, mine], a_loc.at[t])
        return pltpu.make_async_copy(
            x_ref.at[:, :, block_cols(d, t)], raw.at[1, t, mine], a_loc.at[t]
        )

    def forward(side, j, t):
        p = flipped(d, j, nd)
        part = pl.ds(pl.multiple_of(p * layers_here, 8), layers_here)
        if t == tiles:
            src, dst = eb.at[d] if j == 0 else eraw.at[1, part], eraw.at[2 - 2 * side, part]
        else:
            src = x_ref.at[:, :, block_cols(d, t)] if j == 0 else raw.at[1, t, part]
            dst = raw.at[2 - 2 * side, t, part]
        return pltpu.make_async_remote_copy(
            src, dst, z_send.at[side, j, t], z_recv.at[side, j, t],
            device_id={"surf": near[side]}, device_id_type=MESH,
        )

    def forward_both(j, t):
        for side in range(2):
            @pl.when(has[side])
            def _():
                forward(side, j, t).start()

    def heat_out(side):
        return pltpu.make_async_remote_copy(
            heat_ref, hb.at[1 - side], h_send.at[side], h_recv.at[side],
            device_id={"surf": near[side]}, device_id_type=MESH,
        )

    def trade(side, t):
        return pltpu.make_async_remote_copy(
            s2.at[t, pl.ds(2 + 2 * side, 2)], s2.at[t, pl.ds(6 - 6 * side, 2)],
            x_send.at[side, t], x_recv.at[side, t],
            device_id={"surf": near[side]}, device_id_type=MESH,
        )

    def give_back(j, t):
        p = flipped(d, j, nd)
        theirs = pl.ds(pl.multiple_of(p * layers_here, 8), layers_here)
        return pltpu.make_async_remote_copy(
            ob.at[t, theirs], out_ref.at[:, :, block_cols(d, t)],
            o_send.at[j, t], o_recv.at[j, t],
            device_id={"depth": p}, device_id_type=MESH,
        )

    def put_home(t):
        return pltpu.make_async_copy(
            ob.at[t, mine], out_ref.at[:, :, block_cols(d, t)], o_loc.at[t]
        )

    for j in peers:
        spread(j, 0).start()
    forward_both(0, 0)
    lane8 = lax.broadcasted_iota(jnp.int32, (8, LANES), 1)
    for b in range(nd):
        @pl.loop(0, layers_here // 8)
        def _(g):
            rows = pl.ds(pl.multiple_of(g * 8, 8), 8)
            packed = jnp.zeros((8, LANES), jnp.float32)
            for r in range(4):
                edge = jnp.zeros((8, LANES), jnp.float32)
                if b < nd - 1:
                    ahead = x_ref[rows, r, (b + 1) * cols:(b + 1) * cols + LANES]
                    edge = jnp.where(lane8 < REACH, ahead, edge)
                if b > 0:
                    behind = x_ref[rows, r, b * cols - LANES:b * cols]
                    edge = jnp.where(lane8 >= LANES - REACH, behind, edge)
                packed = packed + (pltpu.roll(edge, 16 * r, 1) if r else edge)
            eb[b, rows, :] = packed
    for t in [tiles] + list(range(1, tiles)):
        for j in peers:
            spread(j, t).start()
        forward_both(0, t)
    for t in range(ring):
        keep(t).start()
    for side in range(2):
        @pl.when(has[side])
        def _():
            heat_out(side).start()

    for b in range(layers // LANES):
        row = lab_ref[:, b * LANES:(b + 1) * LANES].astype(jnp.float32)
        tall = jnp.transpose(jnp.broadcast_to(row, (LANES, LANES)))
        lab[b * LANES:(b + 1) * LANES, :] = tall

    @pl.loop(0, layers // 8)
    def _(g):
        rows = pl.ds(pl.multiple_of(g * 8, 8), 8)
        kind = lab[rows, :]
        is0, is1, is2 = kind < 0.5, kind < 1.5, kind < 2.5
        total = jnp.zeros((8, LANES), jnp.float32)
        for k in range(24):
            c = jnp.where(
                is0, nk_ref[0, k],
                jnp.where(is1, nk_ref[1, k], jnp.where(is2, nk_ref[2, k], nk_ref[3, k])),
            )
            coef[k if k < 12 else k + 1, rows, :] = c
            total = total + c
        coef[12, rows, :] = 1.0 - total

    high = op_ref[...].astype(jnp.bfloat16)
    op3[:, 0:layers] = high
    op3[:, layers:2 * layers] = high
    op3[:, 2 * layers:] = (op_ref[...] - high.astype(jnp.float32)).astype(jnp.bfloat16)

    for side in range(2):
        @pl.when(jnp.logical_not(has[side]))
        def _():
            for t in range(ring):
                for r in range(2):
                    s2[t, 6 * side + r, :, :] = jnp.zeros((layers, LANES), jnp.float32)
                for r in range(4):
                    s0[t, 8 * side + r, :, :] = jnp.zeros((layers, LANES), jnp.float32)
            hb[side, :, :] = jnp.zeros((4, width), jnp.float32)

    for side in range(2):
        @pl.when(has[side])
        def _():
            heat_out(side).wait_send()
            heat_out(1 - side).wait_recv()

    row_keep = [jnp.where(h, 1.0, 0.0).astype(jnp.float32) for h in has]
    lane1 = lax.broadcasted_iota(jnp.int32, (1, LANES), 1)
    edge_keep = jnp.where(
        lane1 < REACH, jnp.where(d < nd - 1, 1.0, 0.0),
        jnp.where(lane1 >= LANES - REACH, jnp.where(d > 0, 1.0, 0.0), 0.0),
    ).astype(jnp.float32)

    def heat_row(row, t):
        if row < 0:
            src, r = hb.at[0], row + 4
        elif row > 3:
            src, r = hb.at[1], row - 4
        else:
            src, r = heat_ref, row
        if t < tiles:
            return src[r:r + 1, block_cols(d, t)]
        ahead = src[r:r + 1, block_cols(lax.rem(d + 1, nd), 0)]
        behind = src[r:r + 1, block_cols(lax.rem(d + nd - 1, nd), tiles - 1)]
        return jnp.where(lane1 < REACH, ahead, behind)

    def lateral(src, t, made, first):
        left, right = (t - 1) % ring, (t + 1) % ring

        @pl.loop(0, layers // 8, unroll=2)
        def _(g):
            rows = pl.ds(pl.multiple_of(g * 8, 8), 8)
            acc = [None] * made
            for q in (2, 1, 3, 0, 4):
                cs = [coef[p * 5 + q, rows, :] for p in range(5)]
                for i in range(made + 4):
                    view = src[t, i, rows, :]
                    if q < 2:
                        view = jnp.where(lane8 >= LANES - 2 + q, src[left, i, rows, :], view)
                        view = pltpu.roll(view, 2 - q, 1)
                    elif q > 2:
                        view = jnp.where(lane8 < q - 2, src[right, i, rows, :], view)
                        view = pltpu.roll(view, LANES + 2 - q, 1)
                    for r in range(max(0, i - 4), min(made, i + 1)):
                        term = cs[i - r] * view
                        acc[r] = term if acc[r] is None else acc[r] + term
            for r in range(made):
                ex[rows, r * LANES:(r + 1) * LANES] = acc[r]

        top = lax.broadcasted_iota(jnp.int32, (8, LANES), 0) == 0
        for r in range(made):
            lanes = slice(r * LANES, (r + 1) * LANES)
            heat = jnp.broadcast_to(heat_row(first + r, t), (8, LANES))
            ex[0:8, lanes] = ex[0:8, lanes] + jnp.where(top, heat, 0.0)

    def implicit(t, made, first, store):
        for pair in range(made // 2):
            e = ex[:, pair * 2 * LANES:(pair + 1) * 2 * LANES]
            if first < 0 and pair == 0:
                e = e * row_keep[0]
            if first < 0 and pair == made // 2 - 1:
                e = e * row_keep[1]
            if t == tiles:
                e = e * jnp.concatenate([edge_keep, edge_keep], axis=1)
            eh = e.astype(jnp.bfloat16)
            el = (e - eh.astype(jnp.float32)).astype(jnp.bfloat16)
            y = jnp.dot(
                op3[...], jnp.concatenate([eh, el, eh], axis=0),
                preferred_element_type=jnp.float32,
            )
            store(2 * pair, y[:, :LANES])
            store(2 * pair + 1, y[:, LANES:])

    done = set()
    arrival = [0, tiles] + list(range(1, tiles))

    def once(f):
        def g(t):
            if (f.__name__, t) not in done:
                done.add((f.__name__, t))
                f(t)
        return g

    @once
    def arrive(t):
        at = arrival.index(t)
        if at:
            arrive(arrival[at - 1])
        for j in peers:
            spread(j, t).wait_recv()
            forward_both(j, t)
        keep(t).wait()

    @once
    def unpack(t):
        at = arrival.index(t)
        arrive(arrival[min(at + 1, tiles)])

        def relayout(part):
            if t == tiles:
                @pl.loop(0, layers // 8)
                def _(g):
                    rows = pl.ds(pl.multiple_of(g * 8, 8), 8)
                    packed = eraw[part, rows, :]
                    wanted = jnp.logical_or(lane8 < REACH, lane8 >= LANES - REACH)
                    for r in range(4):
                        v = pltpu.roll(packed, LANES - 16 * r, 1) if r else packed
                        s0[t, 4 * part + r, rows, :] = jnp.where(wanted, v, 0.0)
            else:
                @pl.loop(0, layers // 8)
                def _(g):
                    rows = pl.ds(pl.multiple_of(g * 8, 8), 8)
                    for r in range(4):
                        s0[t, 4 * part + r, rows, :] = raw[part, t, rows, r, :]

        relayout(1)
        for side in range(2):
            @pl.when(has[side])
            def _():
                for j in range(nd):
                    forward(1 - side, j, t).wait_recv()
                relayout(2 * side)

    @once
    def step1(t):
        for u in (t, (t - 1) % ring, (t + 1) % ring):
            unpack(u)
        lateral(s0, t, 8, -2)

        def store(r, y):
            s1[t, r, :, :] = y
        implicit(t, 8, -2, store)

    @once
    def step2(t):
        for u in ((t - 1) % ring, t, (t + 1) % ring):
            step1(u)
        lateral(s1, t, 4, 0)

        def store(r, y):
            s2[t, 2 + r, :, :] = y
        implicit(t, 4, 0, store)
        for side in range(2):
            @pl.when(has[side])
            def _():
                trade(side, t).start()

    @once
    def halo(t):
        for side in range(2):
            @pl.when(has[side])
            def _():
                trade(1 - side, t).wait_recv()

    @once
    def step3(t):
        around = (t, (t - 1) % ring, (t + 1) % ring)
        for u in around:
            step2(u)
        for u in around:
            halo(u)
        lateral(s2, t, 4, 0)

        def store(r, y):
            ob[t, :, r, :] = y
        implicit(t, 4, 0, store)
        for j in peers:
            give_back(j, t).start()
        put_home(t).start()

    order = list(range(1, tiles)) + [0]
    for t in order:
        step3(t)

    for t in order:
        for j in peers:
            give_back(j, t).wait()
        put_home(t).wait()
    for t in range(ring):
        for j in peers:
            spread(j, t).wait_send()
        for side in range(2):
            @pl.when(has[side])
            def _():
                for j in range(nd):
                    forward(side, j, t).wait_send()
                trade(side, t).wait_send()


def shards(
    nd, ns,
    initial_warmth, substance_label, neighbour_kernel, arriving_heat_rate, implicit_inverse_operator,
):
    layers_here, rows, width = initial_warmth.shape
    layers = implicit_inverse_operator.shape[0]
    tiles = width // nd // LANES
    ring = tiles + 1
    labels = substance_label[None, :]
    f32, dma = jnp.float32, pltpu.SemaphoreType.DMA
    vmem = pl.BlockSpec(memory_space=pltpu.VMEM)
    return pl.pallas_call(
        functools.partial(kernel, nd, ns, tiles),
        out_shape=jax.ShapeDtypeStruct(initial_warmth.shape, f32),
        in_specs=[vmem, vmem, pl.BlockSpec(memory_space=pltpu.SMEM), vmem, vmem],
        out_specs=pl.BlockSpec(memory_space=pl.ANY),
        scratch_shapes=[
            pltpu.VMEM((3, tiles, layers, rows, LANES), f32),
            pltpu.VMEM((3, layers, LANES), f32),
            pltpu.VMEM((nd, layers_here, LANES), f32),
            pltpu.VMEM((2, rows, width), f32),
            pltpu.VMEM((ring, 3 * rows, layers, LANES), f32),
            pltpu.VMEM((ring, 2 * rows, layers, LANES), f32),
            pltpu.VMEM((ring, 2 * rows, layers, LANES), f32),
            pltpu.VMEM((layers, 2 * rows * LANES), f32),
            pltpu.VMEM((tiles, layers, rows, LANES), f32),
            pltpu.VMEM((25, layers, LANES), f32),
            pltpu.VMEM((layers, 3 * layers), jnp.bfloat16),
            pltpu.VMEM((layers, LANES), f32),
            dma((nd, ring)), dma((nd, ring)), dma((ring,)),
            dma((2, nd, ring)), dma((2, nd, ring)),
            dma((2,)), dma((2,)), dma((2, ring)), dma((2, ring)),
            dma((nd, tiles)), dma((nd, tiles)), dma((tiles,)),
        ],
        compiler_params=pltpu.CompilerParams(
            collective_id=0, has_side_effects=True, vmem_limit_bytes=60 * 1024 * 1024
        ),
    )(initial_warmth, labels, neighbour_kernel, arriving_heat_rate, implicit_inverse_operator)


def solution(mesh):
    return jax.shard_map(
        functools.partial(shards, mesh.shape["depth"], mesh.shape["surf"]),
        mesh=mesh,
        in_specs=(P("depth", "surf", None), P(), P(), P("surf", None), P()),
        out_specs=P("depth", "surf", None),
        check_vma=False,
    )
```

```python
import functools

import jax
import jax.numpy as jnp
from jax import lax
from jax.experimental import pallas as pl
from jax.experimental.pallas import tpu as pltpu
from jax.sharding import PartitionSpec as P

LANES = 128
REACH = 6
MESH = pl.DeviceIdType.MESH


def flipped(rank, mask, count):
    out, bit = 0, 1
    while bit < count:
        mine = (rank // bit) % 2
        out = out + bit * ((1 - mine) if (mask // bit) % 2 else mine)
        bit *= 2
    return out


def kernel(
    nd, ns, tiles,
    x_ref, lab_ref, nk_ref, heat_ref, op_ref, out_ref,
    raw, eraw, eb, hb, s0, s1, s2, ex, ob, coef, op3, lab,
    a_send, a_recv, a_loc, z_send, z_recv,
    h_send, h_recv, x_send, x_recv, o_send, o_recv, o_loc,
):
    d = lax.axis_index("depth")
    s = lax.axis_index("surf")
    layers_here = x_ref.shape[0]
    layers = op_ref.shape[0]
    width = heat_ref.shape[1]
    cols = tiles * LANES
    ring = tiles + 1
    peers = [j for j in range(nd - 1, 0, -1)]
    has = (s > 0, s < ns - 1)
    near = (s - 1, s + 1)
    mine = pl.ds(pl.multiple_of(d * layers_here, 8), layers_here)

    barrier = pltpu.get_barrier_semaphore()
    for j in peers:
        pl.semaphore_signal(
            barrier, inc=1, device_id={"depth": flipped(d, j, nd)}, device_id_type=MESH
        )
    for side in range(2):
        @pl.when(has[side])
        def _():
            pl.semaphore_signal(
                barrier, inc=1, device_id={"surf": near[side]}, device_id_type=MESH
            )
    at_end = jnp.where(s > 0, 0, 1) + jnp.where(s < ns - 1, 0, 1)
    pl.semaphore_wait(barrier, nd + 1 - at_end)

    def block_cols(b, t):
        return pl.ds(pl.multiple_of(b * cols + t * LANES, LANES), LANES)

    def spread(j, t):
        p = flipped(d, j, nd)
        if t == tiles:
            src, dst = eb.at[p], eraw.at[1, mine]
        else:
            src, dst = x_ref.at[:, :, block_cols(p, t)], raw.at[1, t, mine]
        return pltpu.make_async_remote_copy(
            src, dst, a_send.at[j, t], a_recv.at[j, t],
            device_id={"depth": p}, device_id_type=MESH,
        )

    def keep(t):
        if t == tiles:
            return pltpu.make_async_copy(eb.at[d], eraw.at[1, mine], a_loc.at[t])
        return pltpu.make_async_copy(
            x_ref.at[:, :, block_cols(d, t)], raw.at[1, t, mine], a_loc.at[t]
        )

    def forward(side, j, t):
        p = flipped(d, j, nd)
        part = pl.ds(pl.multiple_of(p * layers_here, 8), layers_here)
        if t == tiles:
            src, dst = eb.at[d] if j == 0 else eraw.at[1, part], eraw.at[2 - 2 * side, part]
        else:
            src = x_ref.at[:, :, block_cols(d, t)] if j == 0 else raw.at[1, t, part]
            dst = raw.at[2 - 2 * side, t, part]
        return pltpu.make_async_remote_copy(
            src, dst, z_send.at[side, j, t], z_recv.at[side, j, t],
            device_id={"surf": near[side]}, device_id_type=MESH,
        )

    def forward_both(j, t):
        for side in range(2):
            @pl.when(has[side])
            def _():
                forward(side, j, t).start()

    def heat_out(side):
        return pltpu.make_async_remote_copy(
            heat_ref, hb.at[1 - side], h_send.at[side], h_recv.at[side],
            device_id={"surf": near[side]}, device_id_type=MESH,
        )

    def trade(side, t):
        return pltpu.make_async_remote_copy(
            s2.at[t, pl.ds(2 + 2 * side, 2)], s2.at[t, pl.ds(6 - 6 * side, 2)],
            x_send.at[side, t], x_recv.at[side, t],
            device_id={"surf": near[side]}, device_id_type=MESH,
        )

    def give_back(j, t):
        p = flipped(d, j, nd)
        theirs = pl.ds(pl.multiple_of(p * layers_here, 8), layers_here)
        return pltpu.make_async_remote_copy(
            ob.at[t, theirs], out_ref.at[:, :, block_cols(d, t)],
            o_send.at[j, t], o_recv.at[j, t],
            device_id={"depth": p}, device_id_type=MESH,
        )

    def put_home(t):
        return pltpu.make_async_copy(
            ob.at[t, mine], out_ref.at[:, :, block_cols(d, t)], o_loc.at[t]
        )

    for j in peers:
        spread(j, 0).start()
    forward_both(0, 0)
    lane8 = lax.broadcasted_iota(jnp.int32, (8, LANES), 1)
    for b in range(nd):
        @pl.loop(0, layers_here // 8)
        def _(g):
            rows = pl.ds(pl.multiple_of(g * 8, 8), 8)
            packed = jnp.zeros((8, LANES), jnp.float32)
            for r in range(4):
                edge = jnp.zeros((8, LANES), jnp.float32)
                if b < nd - 1:
                    ahead = x_ref[rows, r, (b + 1) * cols:(b + 1) * cols + LANES]
                    edge = jnp.where(lane8 < REACH, ahead, edge)
                if b > 0:
                    behind = x_ref[rows, r, b * cols - LANES:b * cols]
                    edge = jnp.where(lane8 >= LANES - REACH, behind, edge)
                packed = packed + (pltpu.roll(edge, 16 * r, 1) if r else edge)
            eb[b, rows, :] = packed
    for t in [tiles] + list(range(1, tiles)):
        for j in peers:
            spread(j, t).start()
        forward_both(0, t)
    for t in range(ring):
        keep(t).start()
    for side in range(2):
        @pl.when(has[side])
        def _():
            heat_out(side).start()

    for b in range(layers // LANES):
        row = lab_ref[:, b * LANES:(b + 1) * LANES].astype(jnp.float32)
        tall = jnp.transpose(jnp.broadcast_to(row, (LANES, LANES)))
        lab[b * LANES:(b + 1) * LANES, :] = tall

    @pl.loop(0, layers // 8)
    def _(g):
        rows = pl.ds(pl.multiple_of(g * 8, 8), 8)
        kind = lab[rows, :]
        is0, is1, is2 = kind < 0.5, kind < 1.5, kind < 2.5
        total = jnp.zeros((8, LANES), jnp.float32)
        for k in range(24):
            c = jnp.where(
                is0, nk_ref[0, k],
                jnp.where(is1, nk_ref[1, k], jnp.where(is2, nk_ref[2, k], nk_ref[3, k])),
            )
            coef[k if k < 12 else k + 1, rows, :] = c
            total = total + c
        coef[12, rows, :] = 1.0 - total

    high = op_ref[...].astype(jnp.bfloat16)
    op3[:, 0:layers] = high
    op3[:, layers:2 * layers] = high
    op3[:, 2 * layers:] = (op_ref[...] - high.astype(jnp.float32)).astype(jnp.bfloat16)

    for side in range(2):
        @pl.when(jnp.logical_not(has[side]))
        def _():
            for t in range(ring):
                for r in range(2):
                    s2[t, 6 * side + r, :, :] = jnp.zeros((layers, LANES), jnp.float32)
                for r in range(4):
                    s0[t, 8 * side + r, :, :] = jnp.zeros((layers, LANES), jnp.float32)
            hb[side, :, :] = jnp.zeros((4, width), jnp.float32)

    for side in range(2):
        @pl.when(has[side])
        def _():
            heat_out(side).wait_send()
            heat_out(1 - side).wait_recv()

    row_keep = [jnp.where(h, 1.0, 0.0).astype(jnp.float32) for h in has]
    lane1 = lax.broadcasted_iota(jnp.int32, (1, LANES), 1)
    edge_keep = jnp.where(
        lane1 < REACH, jnp.where(d < nd - 1, 1.0, 0.0),
        jnp.where(lane1 >= LANES - REACH, jnp.where(d > 0, 1.0, 0.0), 0.0),
    ).astype(jnp.float32)

    def heat_row(row, t):
        if row < 0:
            src, r = hb.at[0], row + 4
        elif row > 3:
            src, r = hb.at[1], row - 4
        else:
            src, r = heat_ref, row
        if t < tiles:
            return src[r:r + 1, block_cols(d, t)]
        ahead = src[r:r + 1, block_cols(lax.rem(d + 1, nd), 0)]
        behind = src[r:r + 1, block_cols(lax.rem(d + nd - 1, nd), tiles - 1)]
        return jnp.where(lane1 < REACH, ahead, behind)

    def lateral(src, t, made, first):
        left, right = (t - 1) % ring, (t + 1) % ring

        @pl.loop(0, layers // 8, unroll=4)
        def _(g):
            rows = pl.ds(pl.multiple_of(g * 8, 8), 8)
            acc = [None] * made
            for q in (2, 1, 3, 0, 4):
                cs = [coef[p * 5 + q, rows, :] for p in range(5)]
                for i in range(made + 4):
                    view = src[t, i, rows, :]
                    if q < 2:
                        view = jnp.where(lane8 >= LANES - 2 + q, src[left, i, rows, :], view)
                        view = pltpu.roll(view, 2 - q, 1)
                    elif q > 2:
                        view = jnp.where(lane8 < q - 2, src[right, i, rows, :], view)
                        view = pltpu.roll(view, LANES + 2 - q, 1)
                    for r in range(max(0, i - 4), min(made, i + 1)):
                        term = cs[i - r] * view
                        acc[r] = term if acc[r] is None else acc[r] + term
            for r in range(made):
                ex[rows, r * LANES:(r + 1) * LANES] = acc[r]

        top = lax.broadcasted_iota(jnp.int32, (8, LANES), 0) == 0
        for r in range(made):
            lanes = slice(r * LANES, (r + 1) * LANES)
            heat = jnp.broadcast_to(heat_row(first + r, t), (8, LANES))
            ex[0:8, lanes] = ex[0:8, lanes] + jnp.where(top, heat, 0.0)

    def implicit(t, made, first, store):
        for pair in range(made // 2):
            e = ex[:, pair * 2 * LANES:(pair + 1) * 2 * LANES]
            if first < 0 and pair == 0:
                e = e * row_keep[0]
            if first < 0 and pair == made // 2 - 1:
                e = e * row_keep[1]
            if t == tiles:
                e = e * jnp.concatenate([edge_keep, edge_keep], axis=1)
            eh = e.astype(jnp.bfloat16)
            el = (e - eh.astype(jnp.float32)).astype(jnp.bfloat16)
            y = jnp.dot(
                op3[...], jnp.concatenate([eh, el, eh], axis=0),
                preferred_element_type=jnp.float32,
            )
            store(2 * pair, y[:, :LANES])
            store(2 * pair + 1, y[:, LANES:])

    done = set()
    arrival = [0, tiles] + list(range(1, tiles))

    def once(f):
        def g(t):
            if (f.__name__, t) not in done:
                done.add((f.__name__, t))
                f(t)
        return g

    @once
    def arrive(t):
        at = arrival.index(t)
        if at:
            arrive(arrival[at - 1])
        for j in peers:
            spread(j, t).wait_recv()
            forward_both(j, t)
        keep(t).wait()

    @once
    def unpack(t):
        at = arrival.index(t)
        arrive(arrival[min(at + 1, tiles)])

        def relayout(part):
            if t == tiles:
                @pl.loop(0, layers // 8)
                def _(g):
                    rows = pl.ds(pl.multiple_of(g * 8, 8), 8)
                    packed = eraw[part, rows, :]
                    wanted = jnp.logical_or(lane8 < REACH, lane8 >= LANES - REACH)
                    for r in range(4):
                        v = pltpu.roll(packed, LANES - 16 * r, 1) if r else packed
                        s0[t, 4 * part + r, rows, :] = jnp.where(wanted, v, 0.0)
            else:
                @pl.loop(0, layers // 8)
                def _(g):
                    rows = pl.ds(pl.multiple_of(g * 8, 8), 8)
                    for r in range(4):
                        s0[t, 4 * part + r, rows, :] = raw[part, t, rows, r, :]

        relayout(1)
        for side in range(2):
            @pl.when(has[side])
            def _():
                for j in range(nd):
                    forward(1 - side, j, t).wait_recv()
                relayout(2 * side)

    @once
    def step1(t):
        for u in (t, (t - 1) % ring, (t + 1) % ring):
            unpack(u)
        lateral(s0, t, 8, -2)

        def store(r, y):
            s1[t, r, :, :] = y
        implicit(t, 8, -2, store)

    @once
    def step2(t):
        for u in ((t - 1) % ring, t, (t + 1) % ring):
            step1(u)
        lateral(s1, t, 4, 0)

        def store(r, y):
            s2[t, 2 + r, :, :] = y
        implicit(t, 4, 0, store)
        for side in range(2):
            @pl.when(has[side])
            def _():
                trade(side, t).start()

    @once
    def halo(t):
        for side in range(2):
            @pl.when(has[side])
            def _():
                trade(1 - side, t).wait_recv()

    @once
    def step3(t):
        around = (t, (t - 1) % ring, (t + 1) % ring)
        for u in around:
            step2(u)
        for u in around:
            halo(u)
        lateral(s2, t, 4, 0)

        def store(r, y):
            ob[t, :, r, :] = y
        implicit(t, 4, 0, store)
        for j in peers:
            give_back(j, t).start()
        put_home(t).start()

    order = list(range(1, tiles)) + [0]
    for t in order:
        step3(t)

    for t in order:
        for j in peers:
            give_back(j, t).wait()
        put_home(t).wait()
    for t in range(ring):
        for j in peers:
            spread(j, t).wait_send()
        for side in range(2):
            @pl.when(has[side])
            def _():
                for j in range(nd):
                    forward(side, j, t).wait_send()
                trade(side, t).wait_send()


def shards(
    nd, ns,
    initial_warmth, substance_label, neighbour_kernel, arriving_heat_rate, implicit_inverse_operator,
):
    layers_here, rows, width = initial_warmth.shape
    layers = implicit_inverse_operator.shape[0]
    tiles = width // nd // LANES
    ring = tiles + 1
    labels = substance_label[None, :]
    f32, dma = jnp.float32, pltpu.SemaphoreType.DMA
    vmem = pl.BlockSpec(memory_space=pltpu.VMEM)
    return pl.pallas_call(
        functools.partial(kernel, nd, ns, tiles),
        out_shape=jax.ShapeDtypeStruct(initial_warmth.shape, f32),
        in_specs=[vmem, vmem, pl.BlockSpec(memory_space=pltpu.SMEM), vmem, vmem],
        out_specs=pl.BlockSpec(memory_space=pl.ANY),
        scratch_shapes=[
            pltpu.VMEM((3, tiles, layers, rows, LANES), f32),
            pltpu.VMEM((3, layers, LANES), f32),
            pltpu.VMEM((nd, layers_here, LANES), f32),
            pltpu.VMEM((2, rows, width), f32),
            pltpu.VMEM((ring, 3 * rows, layers, LANES), f32),
            pltpu.VMEM((ring, 2 * rows, layers, LANES), f32),
            pltpu.VMEM((ring, 2 * rows, layers, LANES), f32),
            pltpu.VMEM((layers, 2 * rows * LANES), f32),
            pltpu.VMEM((tiles, layers, rows, LANES), f32),
            pltpu.VMEM((25, layers, LANES), f32),
            pltpu.VMEM((layers, 3 * layers), jnp.bfloat16),
            pltpu.VMEM((layers, LANES), f32),
            dma((nd, ring)), dma((nd, ring)), dma((ring,)),
            dma((2, nd, ring)), dma((2, nd, ring)),
            dma((2,)), dma((2,)), dma((2, ring)), dma((2, ring)),
            dma((nd, tiles)), dma((nd, tiles)), dma((tiles,)),
        ],
        compiler_params=pltpu.CompilerParams(
            collective_id=0, has_side_effects=True, vmem_limit_bytes=60 * 1024 * 1024
        ),
    )(initial_warmth, labels, neighbour_kernel, arriving_heat_rate, implicit_inverse_operator)


def solution(mesh):
    return jax.shard_map(
        functools.partial(shards, mesh.shape["depth"], mesh.shape["surf"]),
        mesh=mesh,
        in_specs=(P("depth", "surf", None), P(), P(), P("surf", None), P()),
        out_specs=P("depth", "surf", None),
        check_vma=False,
    )
```
